32 devices in a mesh: row: 2 (over y), col: 4 (over z), layer: 4 (over x, core).
Axes of the slice: x: 2, y: 2, z: 4, core: 2. Of those that a mesh axis runs over, the one named last changes fastest.
Arguments:
- density: bfloat16 [128, 4, 128, 128], P(('row', 'col')), may hold values from -1.1953125 to 1.1953125
- tile_cols: int32 [128, 4], replicated, may hold values from 0 to 127, as said below
- out_cols: int32 [128, 4, 4], P(('row', 'col')), may hold values from 0 to 127, as said below
Outputs:
- purified: bfloat16 [128, 4, 4, 128, 128], P(('row', 'col'), 'layer')
The draws below stay inside these ranges and needn't reach their ends.
Inputs may be any that keep to these rules, and one draw needn't show every extreme that they name: Column set l holds the block columns c with (c // 4) % 4 == l; tile_cols[i, l] lies in column set l, so a block row has exactly one tile in each column set. For each i and l, the 4 block columns out_cols[i, l, :] are distinct and lie in column set l.
All inputs are finite; a program needn't handle non-finite values.
Results may differ from the reference program's by a relative error of at most 0.0044.
Values may be sent and summed in bfloat16 or wider, within the bound.
A program may use at most 128 MiB of HBM per device.

```python
import jax
import jax.numpy as jnp
from jax import lax

BS = 128
GROUP_ROWS = 16
KQ = 4
LAYERS = 4
GROUPS = 8
SUB_ROWS = 4
NB = 128


def settle(candidate, earlier):
    shifts = [(candidate + j * GROUP_ROWS) % NB for j in range(KQ)]
    stacked = jnp.stack(shifts, axis=-1)
    if earlier:
        unused = jnp.stack([jnp.all(jnp.stack([shifted != before for before in earlier], axis=0), axis=0) for shifted in shifts], axis=-1)
    else:
        unused = jnp.ones(stacked.shape, dtype=bool)
    chosen_shift = jnp.argmax(unused.astype(jnp.int32), axis=-1)
    return jnp.take_along_axis(stacked, chosen_shift[..., None], axis=-1)[..., 0]


def pattern(key):
    groups_drawn = jax.random.randint(jax.random.fold_in(key, 101), (NB, LAYERS), 0, GROUPS)
    within = jax.random.randint(jax.random.fold_in(key, 202), (NB, LAYERS), 0, SUB_ROWS)
    set_ids = jnp.arange(LAYERS, dtype=jnp.int32)[None, :]
    tile_cols = (groups_drawn * GROUP_ROWS + set_ids * SUB_ROWS + within).astype(jnp.int32)
    set_grid = jnp.arange(LAYERS, dtype=jnp.int32)[None, :, None]
    slot_draw = jax.random.randint(jax.random.fold_in(key, 303), (NB, LAYERS * 2), 0, LAYERS)
    through = jnp.take_along_axis(tile_cols, slot_draw, axis=1).reshape(NB, LAYERS, 2)
    reach_one = tile_cols[through, set_grid]
    slot_zero = settle(reach_one[:, :, 0], [])
    slot_one = settle(reach_one[:, :, 1], [slot_zero])
    base = jnp.stack([slot_zero, slot_one], axis=-1).reshape(NB, LAYERS * 2)
    via_draw = jax.random.randint(jax.random.fold_in(key, 404), (NB, LAYERS * 2), 0, LAYERS * 2)
    through_two = jnp.take_along_axis(base, via_draw, axis=1).reshape(NB, LAYERS, 2)
    reach_two = tile_cols[through_two, set_grid]
    slot_two = settle(reach_two[:, :, 0], [slot_zero, slot_one])
    slot_three = settle(reach_two[:, :, 1], [slot_zero, slot_one, slot_two])
    out_cols = jnp.stack([slot_zero, slot_one, slot_two, slot_three], axis=-1).astype(jnp.int32)
    return (tile_cols, out_cols)


def draw_tile_cols(key, part):
    return pattern(key)[0]


def draw_out_cols(key, part):
    return pattern(key)[1]


def steps_of(key, dims, split, low, top_value):
    factor_of = 1.0
    for axis_at, parts in split:
        heights = jax.random.uniform(jax.random.fold_in(jax.random.fold_in(key, 6), axis_at), (parts,), jnp.float32, low / len(split), top_value / len(split))
        factor_of = factor_of * jnp.repeat(jnp.exp(heights), dims[axis_at] // parts).reshape((-1,) + (1,) * (len(dims) - 1 - axis_at))
    return factor_of


def gaussian(stream_key, dims, width, most, cuts=(), kind=jnp.bfloat16):
    entries = jax.random.normal(stream_key, dims, jnp.float32) * width
    if len(cuts) > 0:
        entries = steps_of(stream_key, dims, cuts, -0.22, 0.18) * entries
    return jnp.clip(entries, min=-most, max=most).astype(kind)


def setup_inputs(seed: int = 0) -> dict:
    streams_of = jax.random.split(jax.random.key(seed), 4)
    density = gaussian(streams_of[0], (NB, LAYERS, BS, BS), 0.2, 1.1953125, ((0, 8),))
    tile_cols = draw_tile_cols(jax.random.fold_in(streams_of[3], 71), 0)
    out_cols = draw_out_cols(jax.random.fold_in(streams_of[3], 71), 0)
    return {"density": density, "tile_cols": tile_cols, "out_cols": out_cols}


def filtered_product(left_tiles, index_tiles, column, colset, wanted):
    step_rows = 32

    def row_block(first_row):
        left_part = lax.dynamic_slice_in_dim(left_tiles, first_row, step_rows, 0).astype(jnp.float32)
        index_part = lax.dynamic_slice_in_dim(index_tiles, first_row, step_rows, 0)
        wanted_part = lax.dynamic_slice_in_dim(wanted, first_row, step_rows, 0)
        b_tiles = jnp.take(column, index_part, axis=0).astype(jnp.float32)
        products = jnp.einsum("imab,imbc->imac", left_part, b_tiles, precision=lax.Precision.HIGHEST)
        matches = (jnp.take(colset, index_part, axis=0)[:, :, None] == wanted_part[:, None, :]).astype(jnp.float32)
        return jnp.einsum("imq,imac->iqac", matches, products, precision=lax.Precision.HIGHEST)

    starts = jnp.arange(left_tiles.shape[0] // step_rows, dtype=jnp.int32) * step_rows
    blocks = lax.map(row_block, starts)
    return blocks.reshape((left_tiles.shape[0],) + blocks.shape[2:])


def reference(density, tile_cols, out_cols):
    layer_ids = jnp.arange(LAYERS, dtype=jnp.int32)

    def square_set(layer_id):
        column = lax.dynamic_index_in_dim(density, layer_id, 1, keepdims=False)
        colset = lax.dynamic_index_in_dim(tile_cols, layer_id, 1, keepdims=False)
        wanted = lax.dynamic_index_in_dim(out_cols, layer_id, 1, keepdims=False)
        return filtered_product(density, tile_cols, column, colset, wanted)

    square = jnp.moveaxis(lax.map(square_set, layer_ids), 0, 1)
    square_low = square.astype(jnp.bfloat16).reshape(NB, LAYERS * KQ, BS, BS)
    cube_index = out_cols.reshape(NB, LAYERS * KQ)

    def purify_set(layer_id):
        column = lax.dynamic_index_in_dim(density, layer_id, 1, keepdims=False)
        colset = lax.dynamic_index_in_dim(tile_cols, layer_id, 1, keepdims=False)
        wanted = lax.dynamic_index_in_dim(out_cols, layer_id, 1, keepdims=False)
        cube = filtered_product(square_low, cube_index, column, colset, wanted)
        own_square = lax.dynamic_index_in_dim(square, layer_id, 1, keepdims=False)
        return (3.0 * own_square - 2.0 * cube).astype(jnp.bfloat16)

    return jnp.moveaxis(lax.map(purify_set, layer_ids), 0, 1)
```

```python
import functools

import jax
import jax.numpy as jnp
from jax import lax
from jax.experimental import pallas as pl
from jax.experimental.pallas import tpu as pltpu
from jax.sharding import PartitionSpec as P

MESH = pl.DeviceIdType.MESH
NT = (((1,), (1,)), ((), ()))


def purify_kernel(
    R, C, L, den_hbm, tc_hbm, oc_hbm, out_hbm, cols, col, den, square, low, result,
    load_sem, out_sem, recv, right_sem, left_sem, far_right, far_left, row_sem,
    recv_low, send_low, relay_low, tc, oc,
):
    own = den_hbm.shape[0]
    bs = den_hbm.shape[2]
    kq = oc_hbm.shape[1]
    pieces, slab = kq, bs // kq
    early = max(own * 3 // 16, 1)
    r, c, l = lax.axis_index("row"), lax.axis_index("col"), lax.axis_index("layer")
    g = r * C + c
    partner = l + 1 - 2 * lax.rem(l, 2)
    rows = [lax.rem(r + d, R) for d in range(1, R)]
    twins = [lax.rem(l + 2 * d, L) for d in range(1, L // 2)]

    own_copy = pltpu.make_async_copy(den_hbm.at[:, l], col.at[pl.ds(g * own, own)], load_sem.at[0])
    own_copy.start()
    den_copy = pltpu.make_async_copy(den_hbm, den, load_sem.at[1])
    den_copy.start()
    tc_copy = pltpu.make_async_copy(tc_hbm, tc, load_sem.at[2])
    tc_copy.start()
    oc_copy = pltpu.make_async_copy(oc_hbm, oc, load_sem.at[3])
    oc_copy.start()

    barrier = pltpu.get_barrier_semaphore()

    def greet(**where):
        pl.semaphore_signal(barrier, inc=1, device_id=where, device_id_type=MESH)

    for other in rows:
        greet(row=other)
    for other in twins + [partner]:
        greet(layer=other)

    @pl.when(c > 0)
    def _():
        greet(col=c - 1)

    @pl.when(c < C - 1)
    def _():
        greet(col=c + 1)

    def turn_own(i, carry):
        tile = col[g * own + i].T
        for p in range(pieces):
            cols[p][g * own + i] = tile[p * slab:(p + 1) * slab]
        return carry

    own_copy.wait()
    lax.fori_loop(0, own, turn_own, 0, unroll=4)
    inner = jnp.where(c > 0, 1, 0) + jnp.where(c < C - 1, 1, 0)
    pl.semaphore_wait(barrier, (R - 1) + (L // 2) + inner)

    def move(group, p, b, sem, where):
        first, count = (early, own - early) if b else (0, early)
        part = cols[p].at[pl.ds(group * own + first, count)]
        return pltpu.make_async_remote_copy(
            src_ref=part,
            dst_ref=part,
            send_sem=sem,
            recv_sem=recv.at[group, p, b],
            device_id=where,
            device_id_type=MESH,
        )

    def arrived(group, p, b):
        move(group, p, b, load_sem.at[0], {"layer": partner}).wait_recv()

    def to_right(group, p, b, sem, act, step=0):
        @pl.when(jnp.minimum(c - step, C - 2 - c) >= 0)
        def _():
            act(move(group, p, b, sem, {"col": c + 1}))

    def to_left(group, p, b, sem, act, step=0):
        @pl.when(jnp.minimum(C - 1 - step - c, c - 1) >= 0)
        def _():
            act(move(group, p, b, sem, {"col": c - 1}))

    def to_rows(group, p, b, at, act):
        for d, other in enumerate(rows):
            act(move(group, p, b, row_sem.at[d, at, p, b], {"row": other}))

    def go(copy):
        copy.start()

    def done(copy):
        copy.wait_send()

    def own_sends(p, act):
        to_rows(g, p, 0, c, act)
        for b in range(2):
            to_right(g, p, b, right_sem.at[c, p, b], act)
            to_left(g, p, b, left_sem.at[c, p, b], act)
        to_rows(g, p, 1, c, act)

    def across(p, act):
        for d, other in enumerate(rows):
            group = other * C + c
            if act is go:
                arrived(group, p, 0)
            to_right(group, p, 0, far_right.at[d, c, p], act)
            to_left(group, p, 0, far_left.at[d, c, p], act)

    def line(p, step, act):
        before = jnp.maximum(c - step, 0)
        after = jnp.minimum(c + step, C - 1)
        for b in range(2):
            @pl.when(c >= step)
            def _():
                if act is go:
                    arrived(r * C + before, p, b)
                if b:
                    to_rows(r * C + before, p, b, before, act)

            to_right(r * C + before, p, b, right_sem.at[before, p, b], act, step)

            @pl.when(c + step < C)
            def _():
                if act is go:
                    arrived(r * C + after, p, b)
                if b:
                    to_rows(r * C + after, p, b, after, act)

            to_left(r * C + after, p, b, left_sem.at[after, p, b], act, step)
        for d, other in enumerate(rows):
            if act is go:
                @pl.when(c >= step)
                def _():
                    arrived(other * C + before, p, 0)
            to_right(other * C + before, p, 0, far_right.at[d, before, p], act, step)
            if act is go:
                @pl.when(c + step < C)
                def _():
                    arrived(other * C + after, p, 0)
            to_left(other * C + after, p, 0, far_left.at[d, after, p], act, step)

    def gather(p):
        across(p, go)
        for step in range(1, C):
            if step == C - 1 and p + 1 < pieces:
                own_sends(p + 1, go)
            line(p, step, go)
        for other in rows:
            for at in range(C):
                arrived(other * C + at, p, 1)

    def low_move(p, u, i, sem, where):
        return pltpu.make_async_remote_copy(
            src_ref=low.at[p, u, i],
            dst_ref=low.at[p, u, i],
            send_sem=sem,
            recv_sem=recv_low.at[p, u, i],
            device_id={"layer": where},
            device_id_type=MESH,
        )

    def low_arrived(p, u, i):
        low_move(p, u, i, load_sem.at[0], partner).wait_recv()

    def send_row(p, i, act):
        for d, other in enumerate(twins + [partner]):
            act(low_move(p, l, i, send_low.at[p, d, i], other))

    def relay(p, i, act):
        for d, other in enumerate(twins):
            if act is go:
                low_arrived(p, other, i)
            act(low_move(p, other, i, relay_low.at[p, d, i], partner))

    def each_row(start, act):
        def step(i, carry):
            act(i)
            return carry

        lax.fori_loop(start, own, step, 0)

    def keep(match, tile):
        return lax.select(match, tile, jnp.zeros_like(tile))

    def square_piece(p):
        def compute(i):
            left = jnp.concatenate([den[i, s] for s in range(L)], axis=1)
            columns = []
            for s in range(L):
                k = tc[s, g * own + i]
                tile = cols[p][k]
                reached = tc[l, k]
                columns.append(
                    jnp.concatenate([keep(reached == oc[l, q, i], tile) for q in range(kq)], axis=0)
                )
            right = jnp.concatenate(columns, axis=1)
            total = lax.dot_general(left, right, NT, preferred_element_type=jnp.float32)
            low[p, l, i] = total.astype(jnp.bfloat16)

        def step(i):
            compute(i)
            send_row(p, i - 1, go)

        compute(0)
        each_row(1, step)
        send_row(p, own - 1, go)

    def turn_back(k, carry):
        col[k] = jnp.concatenate([part[k] for part in cols], axis=0).T
        return carry

    def masked(parts, i):
        columns = [[] for _ in range(kq)]
        for k, tile in parts:
            reached = tc[l, k]
            for q in range(kq):
                columns[q].append(keep(reached == oc[l, q, i], tile))
        return jnp.concatenate([jnp.concatenate(part, axis=0) for part in columns], axis=1)

    def square_row(i):
        left = jnp.concatenate([den[i, s] for s in range(L)], axis=1)
        ks = [tc[s, g * own + i] for s in range(L)]
        right = masked([(k, col[k]) for k in ks], i)
        square[i] = 3.0 * jnp.dot(left, right, preferred_element_type=jnp.float32)

    def cube_row(i):
        for p in range(pieces):
            low_arrived(p, partner, i)
            for other in twins:
                low_arrived(p, other + 1 - 2 * lax.rem(other, 2), i)
        total = jnp.zeros((bs, kq * bs), jnp.float32)
        for p in range(pieces):
            left = jnp.concatenate([low[p, u, i] for u in range(L)], axis=1)
            ks = [oc[u, t, i] for u in range(L) for t in range(kq)]
            right = masked([(k, col[k, p * slab:(p + 1) * slab, :]) for k in ks], i)
            total += jnp.dot(left, right, preferred_element_type=jnp.float32)
        value = (square[i] - 2.0 * total).astype(jnp.bfloat16)
        for q in range(kq):
            result[i, q] = value[:, q * bs:(q + 1) * bs]

    def write(i):
        return pltpu.make_async_copy(result.at[i], out_hbm.at[i, 0], out_sem.at[i])

    own_sends(0, go)
    for p in range(pieces):
        gather(p)
        if p == 0:
            den_copy.wait()
            tc_copy.wait()
            oc_copy.wait()
        square_piece(p)
        if p > 0:
            each_row(0, functools.partial(relay, p - 1, act=go))

    lax.fori_loop(0, R * C * own, turn_back, 0, unroll=4)
    each_row(0, square_row)

    last = pieces - 1
    relay(last, 0, go)

    def cube_step(i):
        relay(last, i, go)
        cube_row(i - 1)

        @pl.when(i > 1)
        def _():
            write(i - 2).start()

    each_row(1, cube_step)
    cube_row(own - 1)
    if own > 1:
        write(own - 2).start()
    write(own - 1).start()

    def finish(i):
        for p in range(pieces):
            send_row(p, i, done)
            relay(p, i, done)
        write(i).wait()

    for p in range(pieces):
        own_sends(p, done)
        across(p, done)
        for step in range(1, C):
            line(p, step, done)
    each_row(0, finish)


def on_device(R, C, L, density, tile_cols, out_cols):
    own, _, bs, _ = density.shape
    kq = out_cols.shape[2]
    pieces = kq
    groups = R * C
    dma = pltpu.SemaphoreType.DMA
    bf16, f32 = jnp.bfloat16, jnp.float32
    tiles = 2 * groups * own + own * L + 2 * own * kq + own * L * kq + own * kq
    vmem = tiles * bs * bs * 2
    tc, oc = tile_cols.T, out_cols.transpose(1, 2, 0)
    return pl.pallas_call(
        functools.partial(purify_kernel, R, C, L),
        out_shape=jax.ShapeDtypeStruct((own, 1, kq, bs, bs), bf16),
        in_specs=[
            pl.BlockSpec(memory_space=pltpu.HBM),
            pl.BlockSpec(memory_space=pltpu.HBM),
            pl.BlockSpec(memory_space=pltpu.HBM),
        ],
        out_specs=pl.BlockSpec(memory_space=pl.ANY),
        scratch_shapes=[
            [pltpu.VMEM((groups * own, bs // pieces, bs), bf16) for _ in range(pieces)],
            pltpu.VMEM((groups * own, bs, bs), bf16),
            pltpu.VMEM((own, L, bs, bs), bf16),
            pltpu.VMEM((own, bs, kq * bs), f32),
            pltpu.VMEM((pieces, L, own, bs, bs), bf16),
            pltpu.VMEM((own, kq, bs, bs), bf16),
            dma((4,)),
            dma((own,)),
            dma((groups, pieces, 2)),
            dma((C, pieces, 2)),
            dma((C, pieces, 2)),
            dma((max(R - 1, 1), C, pieces)),
            dma((max(R - 1, 1), C, pieces)),
            dma((max(R - 1, 1), C, pieces, 2)),
            dma((pieces, L, own)),
            dma((pieces, L // 2, own)),
            dma((pieces, max(L // 2 - 1, 1), own)),
            pltpu.SMEM(tc.shape, jnp.int32),
            pltpu.SMEM(oc.shape, jnp.int32),
        ],
        compiler_params=pltpu.CompilerParams(
            collective_id=0, has_side_effects=True, vmem_limit_bytes=vmem + 2 * 2**20
        ),
    )(density, tc, oc)


def solution(mesh):
    R, C, L = (mesh.shape[name] for name in ("row", "col", "layer"))
    placed = (P(("row", "col"), None, None, None), P(), P(("row", "col"), None, None))
    return jax.shard_map(
        functools.partial(on_device, R, C, L),
        mesh=mesh,
        in_specs=placed,
        out_specs=P(("row", "col"), "layer", None, None, None),
        check_vma=False,
    )
```

```python
import functools

import jax
import jax.numpy as jnp
from jax import lax
from jax.experimental import pallas as pl
from jax.experimental.pallas import tpu as pltpu
from jax.sharding import PartitionSpec as P

MESH = pl.DeviceIdType.MESH
NT = (((1,), (1,)), ((), ()))


def chunk_plan(own):
    early = max(own * 3 // 16, 1)
    late = (own - early + 1) // 2
    return [(0, early), (early, late), (early + late, own - early - late)]


def purify_kernel(
    R, C, L, den_hbm, tc_hbm, oc_hbm, out, cols, col, den, square, low,
    load_sem, recv_early, recv_late, recv_across, right_sem, left_sem, row_sem,
    recv_low, recv_last, send_low, relay_low, tc, oc,
):
    own = den_hbm.shape[0]
    bs = den_hbm.shape[2]
    kq = oc_hbm.shape[1]
    pieces, slab = kq, bs // kq
    last, pair = pieces - 1, 2
    plan = chunk_plan(own)
    early = plan[0][1]
    chunks = range(len(plan))
    r, c, l = lax.axis_index("row"), lax.axis_index("col"), lax.axis_index("layer")
    g = r * C + c
    partner = l + 1 - 2 * lax.rem(l, 2)
    rows = [lax.rem(r + d, R) for d in range(1, R)]
    twins = [lax.rem(l + 2 * d, L) for d in range(1, L // 2)]

    own_copy = pltpu.make_async_copy(den_hbm.at[:, l], col.at[pl.ds(g * own, own)], load_sem.at[0])
    own_copy.start()
    den_copy = pltpu.make_async_copy(den_hbm, den, load_sem.at[1])
    den_copy.start()
    tc_copy = pltpu.make_async_copy(tc_hbm, tc, load_sem.at[2])
    tc_copy.start()
    oc_copy = pltpu.make_async_copy(oc_hbm, oc, load_sem.at[3])
    oc_copy.start()

    barrier = pltpu.get_barrier_semaphore()

    def greet(**where):
        pl.semaphore_signal(barrier, inc=1, device_id=where, device_id_type=MESH)

    for other in rows:
        greet(row=other)
    for other in twins + [partner]:
        greet(layer=other)

    @pl.when(c > 0)
    def _():
        greet(col=c - 1)

    @pl.when(c < C - 1)
    def _():
        greet(col=c + 1)

    def turn_own(i, carry):
        tile = col[g * own + i].T
        for p in range(pieces):
            cols[p][g * own + i] = tile[p * slab:(p + 1) * slab]
        return carry

    own_copy.wait()
    lax.fori_loop(0, own, turn_own, 0, unroll=4)
    inner = jnp.where(c > 0, 1, 0) + jnp.where(c < C - 1, 1, 0)
    pl.semaphore_wait(barrier, (R - 1) + (L // 2) + inner)

    def move(group, p, b, sem, recv, where):
        part = cols[p].at[pl.ds(group * own + plan[b][0], plan[b][1])]
        return pltpu.make_async_remote_copy(
            src_ref=part,
            dst_ref=part,
            send_sem=sem,
            recv_sem=recv,
            device_id=where,
            device_id_type=MESH,
        )

    def landing(row, at, p, b):
        return recv_late.at[at, p, b - 1] if b else recv_early.at[row * C + at, p]

    def arrived(row, at, p, b):
        recv = landing(row, at, p, b)
        move(row * C + at, p, b, right_sem.at[0], recv, {"layer": partner}).wait_recv()

    def to_right(row, at, p, b, step=0):
        @pl.when(jnp.minimum(c - step, C - 2 - c) >= 0)
        def _():
            recv = landing(row, at, p, b)
            move(row * C + at, p, b, right_sem.at[0], recv, {"col": c + 1}).start()

    def to_left(row, at, p, b, step=0):
        @pl.when(jnp.minimum(C - 1 - step - c, c - 1) >= 0)
        def _():
            recv = landing(row, at, p, b)
            move(row * C + at, p, b, left_sem.at[0], recv, {"col": c - 1}).start()

    def to_rows(at, p, b):
        recv = recv_across.at[p] if b else landing(r, at, p, 0)
        for d, other in enumerate(rows):
            move(r * C + at, p, b, row_sem.at[d], recv, {"row": other}).start()

    def own_sends(p):
        to_rows(c, p, 0)
        for b in chunks:
            to_right(r, c, p, b)
            to_left(r, c, p, b)
            if b:
                to_rows(c, p, b)

    def across(p):
        for other in rows:
            arrived(other, c, p, 0)
            to_right(other, c, p, 0)
            to_left(other, c, p, 0)

    def line(p, step):
        before = jnp.maximum(c - step, 0)
        after = jnp.minimum(c + step, C - 1)

        def take(row, b):
            @pl.when(c >= step)
            def _():
                arrived(row, before, p, b)
                if b:
                    to_rows(before, p, b)

            to_right(row, before, p, b, step)

            @pl.when(c + step < C)
            def _():
                arrived(row, after, p, b)
                if b:
                    to_rows(after, p, b)

            to_left(row, after, p, b, step)

        for b in chunks:
            take(r, b)
        for other in rows:
            take(other, 0)

    def begin(p):
        across(p)
        line(p, 1)

    def gather(p):
        for step in range(2, C):
            if step == C - 1 and p < last:
                own_sends(p + 1)
            line(p, step)
        if p < last:
            begin(p + 1)
        part = cols[p].at[pl.ds(0, (R - 1) * C * (own - early))]
        pltpu.make_async_copy(part, part, recv_across.at[p]).wait()

    def sent(sem, tiles):
        part = col.at[pl.ds(0, tiles)]
        pltpu.make_async_copy(part, part, sem).wait()

    def low_move(part, sem, recv, where):
        return pltpu.make_async_remote_copy(
            src_ref=part,
            dst_ref=part,
            send_sem=sem,
            recv_sem=recv,
            device_id={"layer": where},
            device_id_type=MESH,
        )

    def low_rows(p, u, j):
        return low.at[u, p, pl.ds(j * pair, pair)]

    def low_landing(p, u, j):
        return recv_last.at[u, j] if p == last else recv_low.at[p, u]

    def low_arrived(p, u, j=None):
        part = low.at[u, p] if j is None else low_rows(p, u, j)
        low_move(part, right_sem.at[0], low_landing(p, u, j), partner).wait_recv()

    def send_rows(p, j):
        for d, other in enumerate(twins + [partner]):
            low_move(low_rows(p, l, j), send_low.at[d], low_landing(p, l, j), other).start()

    def relay(p, j=None):
        for d, other in enumerate(twins):
            low_arrived(p, other, j)
            part = low.at[other, p] if j is None else low_rows(p, other, j)
            low_move(part, relay_low.at[d], low_landing(p, other, j), partner).start()

    def each(start, count, act):
        def step(i, carry):
            act(i)
            return carry

        lax.fori_loop(start, count, step, 0)

    def keep(match, tile):
        return lax.select(match, tile, jnp.zeros_like(tile))

    def square_piece(p):
        def compute(i):
            left = jnp.concatenate([den[i, s] for s in range(L)], axis=1)
            columns = []
            for s in range(L):
                k = tc[s, g * own + i]
                tile = cols[p][k]
                reached = tc[l, k]
                columns.append(
                    jnp.concatenate([keep(reached == oc[l, q, i], tile) for q in range(kq)], axis=0)
                )
            right = jnp.concatenate(columns, axis=1)
            total = lax.dot_general(left, right, NT, preferred_element_type=jnp.float32)
            low[l, p, i] = total.astype(jnp.bfloat16)

        def both(j):
            for i in range(pair):
                compute(j * pair + i)

        def step(j):
            both(j)
            send_rows(p, j - 1)

        both(0)
        each(1, own // pair, step)
        send_rows(p, own // pair - 1)

    def turn_back(k, carry):
        col[k] = jnp.concatenate([part[k] for part in cols], axis=0).T
        return carry

    def masked(parts, i):
        columns = [[] for _ in range(kq)]
        for k, tile in parts:
            reached = tc[l, k]
            for q in range(kq):
                columns[q].append(keep(reached == oc[l, q, i], tile))
        return jnp.concatenate([jnp.concatenate(part, axis=0) for part in columns], axis=1)

    def square_row(i):
        left = jnp.concatenate([den[i, s] for s in range(L)], axis=1)
        ks = [tc[s, g * own + i] for s in range(L)]
        right = masked([(k, col[k]) for k in ks], i)
        square[i] = 3.0 * jnp.dot(left, right, preferred_element_type=jnp.float32)

    def cube_row(i):
        total = jnp.zeros((bs, kq * bs), jnp.float32)
        for p in range(pieces):
            left = jnp.concatenate([low[u, p, i] for u in range(L)], axis=1)
            ks = [oc[u, t, i] for u in range(L) for t in range(kq)]
            right = masked([(k, col[k, p * slab:(p + 1) * slab, :]) for k in ks], i)
            total += jnp.dot(left, right, preferred_element_type=jnp.float32)
        value = (square[i] - 2.0 * total).astype(jnp.bfloat16)
        for q in range(kq):
            out[i, 0, q] = value[:, q * bs:(q + 1) * bs]

    own_sends(0)
    begin(0)
    for p in range(pieces):
        gather(p)
        if p == 0:
            den_copy.wait()
            tc_copy.wait()
            oc_copy.wait()
        square_piece(p)
        if p > 1:
            relay(p - 2)

    lax.fori_loop(0, R * C * own, turn_back, 0, unroll=4)
    each(0, own, square_row)
    relay(last - 1)
    others = [partner] + [other + 1 - 2 * lax.rem(other, 2) for other in twins]
    for p in range(last):
        for other in others:
            low_arrived(p, other)

    def cube_rows(j):
        for other in others:
            low_arrived(last, other, j)
        for i in range(pair):
            cube_row(j * pair + i)

    def cube_step(j):
        relay(last, j)
        cube_rows(j - 1)

    relay(last, 0)
    each(1, own // pair, cube_step)
    cube_rows(own // pair - 1)

    for at in range(C - 1):
        tiles = (at + 1) * (own + (R - 1) * early)

        @pl.when(c == at)
        def _():
            sent(right_sem.at[0], tiles)

        @pl.when(C - 1 - c == at)
        def _():
            sent(left_sem.at[0], tiles)

    for d in range(R - 1):
        sent(row_sem.at[d], own + (C - 1) * (own - early))
    for d, other in enumerate(twins + [partner]):
        low_move(low.at[l], send_low.at[d], recv_low.at[0, 0], other).wait_send()
    for d, other in enumerate(twins):
        low_move(low.at[other], relay_low.at[d], recv_low.at[0, 0], partner).wait_send()


def on_device(R, C, L, density, tile_cols, out_cols):
    own, _, bs, _ = density.shape
    kq = out_cols.shape[2]
    pieces = kq
    groups = R * C
    chunks = len(chunk_plan(own))
    dma = pltpu.SemaphoreType.DMA
    bf16, f32 = jnp.bfloat16, jnp.float32
    tc, oc = tile_cols.T, out_cols.transpose(1, 2, 0)
    return pl.pallas_call(
        functools.partial(purify_kernel, R, C, L),
        out_shape=jax.ShapeDtypeStruct((own, 1, kq, bs, bs), bf16),
        in_specs=[
            pl.BlockSpec(memory_space=pltpu.HBM),
            pl.BlockSpec(memory_space=pltpu.HBM),
            pl.BlockSpec(memory_space=pltpu.HBM),
        ],
        out_specs=pl.BlockSpec(memory_space=pltpu.VMEM),
        scratch_shapes=[
            [pltpu.VMEM((groups * own, bs // pieces, bs), bf16) for _ in range(pieces)],
            pltpu.VMEM((groups * own, bs, bs), bf16),
            pltpu.VMEM((own, L, bs, bs), bf16),
            pltpu.VMEM((own, bs, kq * bs), f32),
            pltpu.VMEM((L, pieces, own, bs, bs), bf16),
            dma((4,)),
            dma((groups, pieces)),
            dma((C, pieces, chunks - 1)),
            dma((pieces,)),
            dma((1,)),
            dma((1,)),
            dma((max(R - 1, 1),)),
            dma((pieces - 1, L)),
            dma((L, own // 2)),
            dma((L // 2,)),
            dma((max(L // 2 - 1, 1),)),
            pltpu.SMEM(tc.shape, jnp.int32),
            pltpu.SMEM(oc.shape, jnp.int32),
        ],
        compiler_params=pltpu.CompilerParams(
            collective_id=0, has_side_effects=True, vmem_limit_bytes=60 * 2**20
        ),
    )(density, tc, oc)


def solution(mesh):
    R, C, L = (mesh.shape[name] for name in ("row", "col", "layer"))
    placed = (P(("row", "col"), None, None, None), P(), P(("row", "col"), None, None))
    return jax.shard_map(
        functools.partial(on_device, R, C, L),
        mesh=mesh,
        in_specs=placed,
        out_specs=P(("row", "col"), "layer", None, None, None),
        check_vma=False,
    )
```

```python
import functools

import jax
import jax.numpy as jnp
from jax import lax
from jax.experimental import pallas as pl
from jax.experimental.pallas import tpu as pltpu
from jax.sharding import PartitionSpec as P

MESH = pl.DeviceIdType.MESH
NT = (((1,), (1,)), ((), ()))


def chunk_plan(own):
    early = max(own * 3 // 16, 1)
    late = (own - early + 1) // 2
    return [(0, early), (early, late), (early + late, own - early - late)]


def purify_kernel(
    R, C, L, den_hbm, tc_hbm, oc_hbm, out, cols, col, den, square, low,
    load_sem, recv_early, recv_late, recv_across, right_sem, left_sem, row_sem,
    recv_low, recv_last, send_low, relay_low, tc, oc,
):
    own = den_hbm.shape[0]
    bs = den_hbm.shape[2]
    kq = oc_hbm.shape[1]
    pieces, slab = kq, bs // kq
    last, pair = pieces - 1, 2
    plan = chunk_plan(own)
    early = plan[0][1]
    chunks = range(len(plan))
    r, c, l = lax.axis_index("row"), lax.axis_index("col"), lax.axis_index("layer")
    g = r * C + c
    partner = l + 1 - 2 * lax.rem(l, 2)
    rows = [lax.rem(r + d, R) for d in range(1, R)]
    twins = [lax.rem(l + 2 * d, L) for d in range(1, L // 2)]

    own_copy = pltpu.make_async_copy(den_hbm.at[:, l], col.at[pl.ds(g * own, own)], load_sem.at[0])
    own_copy.start()
    den_copy = pltpu.make_async_copy(den_hbm, den, load_sem.at[1])
    den_copy.start()
    tc_copy = pltpu.make_async_copy(tc_hbm, tc, load_sem.at[2])
    tc_copy.start()
    oc_copy = pltpu.make_async_copy(oc_hbm, oc, load_sem.at[3])
    oc_copy.start()

    barrier = pltpu.get_barrier_semaphore()

    def greet(**where):
        pl.semaphore_signal(barrier, inc=1, device_id=where, device_id_type=MESH)

    for other in rows:
        greet(row=other)
    for other in twins + [partner]:
        greet(layer=other)

    @pl.when(c > 0)
    def _():
        greet(col=c - 1)

    @pl.when(c < C - 1)
    def _():
        greet(col=c + 1)

    def turn_own(i, carry):
        tile = col[g * own + i].T
        for p in range(pieces):
            cols[p][g * own + i] = tile[p * slab:(p + 1) * slab]
        return carry

    own_copy.wait()
    lax.fori_loop(0, own, turn_own, 0, unroll=4)
    inner = jnp.where(c > 0, 1, 0) + jnp.where(c < C - 1, 1, 0)
    pl.semaphore_wait(barrier, (R - 1) + (L // 2) + inner)

    def move(group, p, b, sem, recv, where):
        part = cols[p].at[pl.ds(group * own + plan[b][0], plan[b][1])]
        return pltpu.make_async_remote_copy(
            src_ref=part,
            dst_ref=part,
            send_sem=sem,
            recv_sem=recv,
            device_id=where,
            device_id_type=MESH,
        )

    def landing(row, at, p, b):
        return recv_late.at[at, p, b - 1] if b else recv_early.at[row * C + at, p]

    def arrived(row, at, p, b):
        recv = landing(row, at, p, b)
        move(row * C + at, p, b, right_sem.at[0], recv, {"layer": partner}).wait_recv()

    def to_right(row, at, p, b, step=0):
        @pl.when(jnp.minimum(c - step, C - 2 - c) >= 0)
        def _():
            recv = landing(row, at, p, b)
            move(row * C + at, p, b, right_sem.at[0], recv, {"col": c + 1}).start()

    def to_left(row, at, p, b, step=0):
        @pl.when(jnp.minimum(C - 1 - step - c, c - 1) >= 0)
        def _():
            recv = landing(row, at, p, b)
            move(row * C + at, p, b, left_sem.at[0], recv, {"col": c - 1}).start()

    def to_rows(at, p, b):
        recv = recv_across.at[p] if b else landing(r, at, p, 0)
        for d, other in enumerate(rows):
            move(r * C + at, p, b, row_sem.at[d], recv, {"row": other}).start()

    def own_sends(p):
        to_rows(c, p, 0)
        for b in chunks:
            to_right(r, c, p, b)
            to_left(r, c, p, b)
            if b:
                to_rows(c, p, b)

    def across(p):
        for other in rows:
            arrived(other, c, p, 0)
            to_right(other, c, p, 0)
            to_left(other, c, p, 0)

    def line(p, step):
        before = jnp.maximum(c - step, 0)
        after = jnp.minimum(c + step, C - 1)

        def take(row, b):
            @pl.when(c >= step)
            def _():
                arrived(row, before, p, b)
                if b:
                    to_rows(before, p, b)

            to_right(row, before, p, b, step)

            @pl.when(c + step < C)
            def _():
                arrived(row, after, p, b)
                if b:
                    to_rows(after, p, b)

            to_left(row, after, p, b, step)

        for b in chunks:
            take(r, b)
        for other in rows:
            take(other, 0)

    def begin(p):
        across(p)
        line(p, 1)

    def middle(p):
        for step in range(2, C - 1):
            line(p, step)

    def ending(p):
        if p < last:
            own_sends(p + 1)
        if C > 2:
            line(p, C - 1)
        if p < last:
            begin(p + 1)
        part = cols[p].at[pl.ds(0, (R - 1) * C * (own - early))]
        pltpu.make_async_copy(part, part, recv_across.at[p]).wait()

    def sent(sem, tiles):
        part = col.at[pl.ds(0, tiles)]
        pltpu.make_async_copy(part, part, sem).wait()

    def low_move(part, sem, recv, where):
        return pltpu.make_async_remote_copy(
            src_ref=part,
            dst_ref=part,
            send_sem=sem,
            recv_sem=recv,
            device_id={"layer": where},
            device_id_type=MESH,
        )

    def low_rows(p, u, j):
        return low.at[u, p, pl.ds(j * pair, pair)]

    def low_landing(p, u, j):
        return recv_last.at[u, j] if p == last else recv_low.at[p, u]

    def low_arrived(p, u, j=None):
        part = low.at[u, p] if j is None else low_rows(p, u, j)
        low_move(part, right_sem.at[0], low_landing(p, u, j), partner).wait_recv()

    def send_rows(p, j):
        for d, other in enumerate(twins + [partner]):
            low_move(low_rows(p, l, j), send_low.at[d], low_landing(p, l, j), other).start()

    def relay(p, j=None):
        for d, other in enumerate(twins):
            low_arrived(p, other, j)
            part = low.at[other, p] if j is None else low_rows(p, other, j)
            low_move(part, relay_low.at[d], low_landing(p, other, j), partner).start()

    def each(start, count, act):
        def step(i, carry):
            act(i)
            return carry

        lax.fori_loop(start, count, step, 0)

    def keep(match, tile):
        return lax.select(match, tile, jnp.zeros_like(tile))

    def square_piece(p, first, count):
        def compute(i):
            left = jnp.concatenate([den[i, s] for s in range(L)], axis=1)
            columns = []
            for s in range(L):
                k = tc[s, g * own + i]
                tile = cols[p][k]
                reached = tc[l, k]
                columns.append(
                    jnp.concatenate([keep(reached == oc[l, q, i], tile) for q in range(kq)], axis=0)
                )
            right = jnp.concatenate(columns, axis=1)
            total = lax.dot_general(left, right, NT, preferred_element_type=jnp.float32)
            low[l, p, i] = total.astype(jnp.bfloat16)
            for q in range(kq):
                part = slice(q * bs + p * slab, q * bs + (p + 1) * slab)
                square[i, :, part] = total[:, q * slab:(q + 1) * slab]

        def both(j):
            for i in range(pair):
                compute(j * pair + i)

        def step(j):
            both(j)
            send_rows(p, j - 1)

        both(first)
        each(first + 1, count, step)
        send_rows(p, count - 1)

    def turn_back(k, carry):
        col[k] = jnp.concatenate([part[k] for part in cols], axis=0).T
        return carry

    def masked(parts, i):
        columns = [[] for _ in range(kq)]
        for k, tile in parts:
            reached = tc[l, k]
            for q in range(kq):
                columns[q].append(keep(reached == oc[l, q, i], tile))
        return jnp.concatenate([jnp.concatenate(part, axis=0) for part in columns], axis=1)

    def cube(i):
        total = jnp.zeros((bs, kq * bs), jnp.float32)
        for p in range(pieces):
            left = jnp.concatenate([low[u, p, i] for u in range(L)], axis=1)
            ks = [oc[u, t, i] for u in range(L) for t in range(kq)]
            right = masked([(k, col[k, p * slab:(p + 1) * slab, :]) for k in ks], i)
            total += jnp.dot(left, right, preferred_element_type=jnp.float32)
        return 2.0 * total

    def cube_row(i):
        value = (3.0 * square[i] - cube(i)).astype(jnp.bfloat16)
        for q in range(kq):
            out[i, 0, q] = value[:, q * bs:(q + 1) * bs]

    own_sends(0)
    begin(0)
    middle(0)
    ending(0)
    den_copy.wait()
    tc_copy.wait()
    oc_copy.wait()
    half = own // pair // 2
    for p in range(pieces):
        square_piece(p, 0, half)
        if p < last:
            middle(p + 1)
        square_piece(p, half, own // pair)
        if p > 1:
            relay(p - 2)
        if p < last:
            ending(p + 1)

    lax.fori_loop(0, R * C * own, turn_back, 0, unroll=4)
    relay(last - 1)
    others = [partner] + [other + 1 - 2 * lax.rem(other, 2) for other in twins]
    for p in range(last):
        for other in others:
            low_arrived(p, other)

    def cube_rows(j):
        for other in others:
            low_arrived(last, other, j)
        for i in range(pair):
            cube_row(j * pair + i)

    def cube_step(j):
        relay(last, j)
        cube_rows(j - 1)

    relay(last, 0)
    each(1, own // pair, cube_step)
    cube_rows(own // pair - 1)

    for at in range(C - 1):
        tiles = (at + 1) * (own + (R - 1) * early)

        @pl.when(c == at)
        def _():
            sent(right_sem.at[0], tiles)

        @pl.when(C - 1 - c == at)
        def _():
            sent(left_sem.at[0], tiles)

    for d in range(R - 1):
        sent(row_sem.at[d], own + (C - 1) * (own - early))
    for d, other in enumerate(twins + [partner]):
        low_move(low.at[l], send_low.at[d], recv_low.at[0, 0], other).wait_send()
    for d, other in enumerate(twins):
        low_move(low.at[other], relay_low.at[d], recv_low.at[0, 0], partner).wait_send()


def on_device(R, C, L, density, tile_cols, out_cols):
    own, _, bs, _ = density.shape
    kq = out_cols.shape[2]
    pieces = kq
    groups = R * C
    chunks = len(chunk_plan(own))
    dma = pltpu.SemaphoreType.DMA
    bf16, f32 = jnp.bfloat16, jnp.float32
    tiles = 2 * groups * own + own * L + 2 * own * kq + own * L * kq + own * kq
    vmem = tiles * bs * bs * 2 + 2 * 2**20
    tc, oc = tile_cols.T, out_cols.transpose(1, 2, 0)
    return pl.pallas_call(
        functools.partial(purify_kernel, R, C, L),
        out_shape=jax.ShapeDtypeStruct((own, 1, kq, bs, bs), bf16),
        in_specs=[
            pl.BlockSpec(memory_space=pltpu.HBM),
            pl.BlockSpec(memory_space=pltpu.HBM),
            pl.BlockSpec(memory_space=pltpu.HBM),
        ],
        out_specs=pl.BlockSpec(memory_space=pltpu.VMEM),
        scratch_shapes=[
            [pltpu.VMEM((groups * own, bs // pieces, bs), bf16) for _ in range(pieces)],
            pltpu.VMEM((groups * own, bs, bs), bf16),
            pltpu.VMEM((own, L, bs, bs), bf16),
            pltpu.VMEM((own, bs, kq * bs), f32),
            pltpu.VMEM((L, pieces, own, bs, bs), bf16),
            dma((4,)),
            dma((groups, pieces)),
            dma((C, pieces, chunks - 1)),
            dma((pieces,)),
            dma((1,)),
            dma((1,)),
            dma((max(R - 1, 1),)),
            dma((pieces - 1, L)),
            dma((L, own // 2)),
            dma((L // 2,)),
            dma((max(L // 2 - 1, 1),)),
            pltpu.SMEM(tc.shape, jnp.int32),
            pltpu.SMEM(oc.shape, jnp.int32),
        ],
        compiler_params=pltpu.CompilerParams(
            collective_id=0, has_side_effects=True, vmem_limit_bytes=max(vmem, 51 * 2**20)
        ),
    )(density, tc, oc)


def solution(mesh):
    R, C, L = (mesh.shape[name] for name in ("row", "col", "layer"))
    placed = (P(("row", "col"), None, None, None), P(), P(("row", "col"), None, None))
    return jax.shard_map(
        functools.partial(on_device, R, C, L),
        mesh=mesh,
        in_specs=placed,
        out_specs=P(("row", "col"), "layer", None, None, None),
        check_vma=False,
    )
```

```python
import functools

import jax
import jax.numpy as jnp
from jax import lax
from jax.experimental import pallas as pl
from jax.experimental.pallas import tpu as pltpu
from jax.sharding import PartitionSpec as P

MESH = pl.DeviceIdType.MESH
NT = (((1,), (1,)), ((), ()))


def chunk_plan(own):
    early = max(own * 3 // 16, 1)
    late = (own - early + 1) // 2
    return [(0, early), (early, late), (early + late, own - early - late)]


def purify_kernel(
    R, C, L, den_hbm, tc_hbm, oc_hbm, out, cols, col, den, square, low,
    load_sem, recv_early, recv_late, recv_across, right_sem, left_sem, row_sem,
    recv_low, recv_last, send_low, relay_low, tc, oc,
):
    own = den_hbm.shape[0]
    bs = den_hbm.shape[2]
    kq = oc_hbm.shape[1]
    pieces, slab = kq, bs // kq
    last, pair = pieces - 1, 2
    plan = chunk_plan(own)
    early = plan[0][1]
    chunks = range(len(plan))
    r, c, l = lax.axis_index("row"), lax.axis_index("col"), lax.axis_index("layer")
    g = r * C + c
    partner = l + 1 - 2 * lax.rem(l, 2)
    rows = [lax.rem(r + d, R) for d in range(1, R)]
    twins = [lax.rem(l + 2 * d, L) for d in range(1, L // 2)]

    own_copy = pltpu.make_async_copy(den_hbm.at[:, l], col.at[pl.ds(g * own, own)], load_sem.at[0])
    own_copy.start()
    den_copy = pltpu.make_async_copy(den_hbm, den, load_sem.at[1])
    den_copy.start()
    tc_copy = pltpu.make_async_copy(tc_hbm, tc, load_sem.at[2])
    tc_copy.start()
    oc_copy = pltpu.make_async_copy(oc_hbm, oc, load_sem.at[3])
    oc_copy.start()

    barrier = pltpu.get_barrier_semaphore()

    def greet(**where):
        pl.semaphore_signal(barrier, inc=1, device_id=where, device_id_type=MESH)

    for other in rows:
        greet(row=other)
    for other in twins + [partner]:
        greet(layer=other)

    @pl.when(c > 0)
    def _():
        greet(col=c - 1)

    @pl.when(c < C - 1)
    def _():
        greet(col=c + 1)

    def turn_own(i, carry):
        tile = col[g * own + i].T
        for p in range(pieces):
            cols[p][g * own + i] = tile[p * slab:(p + 1) * slab]
        return carry

    own_copy.wait()
    lax.fori_loop(0, own, turn_own, 0, unroll=4)
    inner = jnp.where(c > 0, 1, 0) + jnp.where(c < C - 1, 1, 0)
    pl.semaphore_wait(barrier, (R - 1) + (L // 2) + inner)

    def move(group, p, b, sem, recv, where):
        part = cols[p].at[pl.ds(group * own + plan[b][0], plan[b][1])]
        return pltpu.make_async_remote_copy(
            src_ref=part,
            dst_ref=part,
            send_sem=sem,
            recv_sem=recv,
            device_id=where,
            device_id_type=MESH,
        )

    def landing(row, at, p, b):
        return recv_late.at[at, p, b - 1] if b else recv_early.at[row * C + at, p]

    def arrived(row, at, p, b):
        recv = landing(row, at, p, b)
        move(row * C + at, p, b, right_sem.at[0], recv, {"layer": partner}).wait_recv()

    def to_right(row, at, p, b, step=0):
        @pl.when(jnp.minimum(c - step, C - 2 - c) >= 0)
        def _():
            recv = landing(row, at, p, b)
            move(row * C + at, p, b, right_sem.at[0], recv, {"col": c + 1}).start()

    def to_left(row, at, p, b, step=0):
        @pl.when(jnp.minimum(C - 1 - step - c, c - 1) >= 0)
        def _():
            recv = landing(row, at, p, b)
            move(row * C + at, p, b, left_sem.at[0], recv, {"col": c - 1}).start()

    def to_rows(at, p, b):
        recv = recv_across.at[p] if b else landing(r, at, p, 0)
        for d, other in enumerate(rows):
            move(r * C + at, p, b, row_sem.at[d], recv, {"row": other}).start()

    def own_sends(p):
        to_rows(c, p, 0)
        for b in chunks:
            to_right(r, c, p, b)
            to_left(r, c, p, b)
            if b:
                to_rows(c, p, b)

    def across(p):
        for other in rows:
            arrived(other, c, p, 0)
            to_right(other, c, p, 0)
            to_left(other, c, p, 0)

    def line(p, step):
        before = jnp.maximum(c - step, 0)
        after = jnp.minimum(c + step, C - 1)

        def take(row, b):
            @pl.when(c >= step)
            def _():
                arrived(row, before, p, b)
                if b:
                    to_rows(before, p, b)

            to_right(row, before, p, b, step)

            @pl.when(c + step < C)
            def _():
                arrived(row, after, p, b)
                if b:
                    to_rows(after, p, b)

            to_left(row, after, p, b, step)

        for b in chunks:
            take(r, b)
        for other in rows:
            take(other, 0)

    def begin(p):
        across(p)
        line(p, 1)

    def middle(p):
        for step in range(2, C - 1):
            line(p, step)

    def ending(p):
        if p < last:
            own_sends(p + 1)
        if C > 2:
            line(p, C - 1)
        if p < last:
            begin(p + 1)
        part = cols[p].at[pl.ds(0, (R - 1) * C * (own - early))]
        pltpu.make_async_copy(part, part, recv_across.at[p]).wait()

    def sent(sem, tiles):
        part = col.at[pl.ds(0, tiles)]
        pltpu.make_async_copy(part, part, sem).wait()

    def low_move(part, sem, recv, where):
        return pltpu.make_async_remote_copy(
            src_ref=part,
            dst_ref=part,
            send_sem=sem,
            recv_sem=recv,
            device_id={"layer": where},
            device_id_type=MESH,
        )

    def low_rows(p, u, j):
        return low.at[u, p, pl.ds(j * pair, pair)]

    def low_landing(p, u, j):
        return recv_last.at[u, j] if p == last else recv_low.at[p, u]

    def low_arrived(p, u, j=None):
        part = low.at[u, p] if j is None else low_rows(p, u, j)
        low_move(part, right_sem.at[0], low_landing(p, u, j), partner).wait_recv()

    def send_rows(p, j):
        for d, other in enumerate(twins + [partner]):
            low_move(low_rows(p, l, j), send_low.at[d], low_landing(p, l, j), other).start()

    def relay(p, j=None):
        for d, other in enumerate(twins):
            low_arrived(p, other, j)
            part = low.at[other, p] if j is None else low_rows(p, other, j)
            low_move(part, relay_low.at[d], low_landing(p, other, j), partner).start()

    def each(start, count, act):
        def step(i, carry):
            act(i)
            return carry

        lax.fori_loop(start, count, step, 0)

    def keep(match, tile):
        return lax.select(match, tile, jnp.zeros_like(tile))

    def square_piece(p, first, count):
        def compute(i):
            left = jnp.concatenate([den[i, s] for s in range(L)], axis=1)
            columns = []
            for s in range(L):
                k = tc[s, g * own + i]
                tile = cols[p][k]
                reached = tc[l, k]
                columns.append(
                    jnp.concatenate([keep(reached == oc[l, q, i], tile) for q in range(kq)], axis=0)
                )
            right = jnp.concatenate(columns, axis=1)
            total = lax.dot_general(left, right, NT, preferred_element_type=jnp.float32)
            low[l, p, i] = total.astype(jnp.bfloat16)
            for q in range(kq):
                part = slice(q * bs + p * slab, q * bs + (p + 1) * slab)
                square[i, :, part] = total[:, q * slab:(q + 1) * slab]

        def both(j):
            for i in range(pair):
                compute(j * pair + i)

        def step(j):
            both(j)
            send_rows(p, j - 1)

        both(first)
        each(first + 1, count, step)
        send_rows(p, count - 1)

    def turn_back(k, carry):
        col[k] = jnp.concatenate([part[k] for part in cols], axis=0).T
        return carry

    def masked(parts, i):
        columns = [[] for _ in range(kq)]
        for k, tile in parts:
            reached = tc[l, k]
            for q in range(kq):
                columns[q].append(keep(reached == oc[l, q, i], tile))
        return jnp.concatenate([jnp.concatenate(part, axis=0) for part in columns], axis=1)

    def cube(i):
        total = jnp.zeros((bs, kq * bs), jnp.float32)
        for p in range(pieces):
            left = jnp.concatenate([low[u, p, i] for u in range(L)], axis=1)
            ks = [oc[u, t, i] for u in range(L) for t in range(kq)]
            right = masked([(k, col[k, p * slab:(p + 1) * slab, :]) for k in ks], i)
            total += jnp.dot(left, right, preferred_element_type=jnp.float32)
        return 2.0 * total

    def cube_row(i):
        value = (3.0 * square[i] - cube(i)).astype(jnp.bfloat16)
        for q in range(kq):
            out[i, 0, q] = value[:, q * bs:(q + 1) * bs]

    own_sends(0)
    begin(0)
    middle(0)
    ending(0)
    den_copy.wait()
    tc_copy.wait()
    oc_copy.wait()
    half = own // pair // 2
    for p in range(pieces):
        square_piece(p, 0, half)
        if p < last:
            middle(p + 1)
        square_piece(p, half, own // pair)
        if p > 1:
            relay(p - 2)
        if p < last:
            ending(p + 1)

    lax.fori_loop(0, R * C * own, turn_back, 0, unroll=4)
    relay(last - 1)
    others = [partner] + [other + 1 - 2 * lax.rem(other, 2) for other in twins]
    for p in range(last):
        for other in others:
            low_arrived(p, other)

    def cube_rows(j):
        for other in others:
            low_arrived(last, other, j)
        for i in range(pair):
            cube_row(j * pair + i)

    def cube_step(j):
        relay(last, j)
        cube_rows(j - 1)

    relay(last, 0)
    each(1, own // pair, cube_step)
    cube_rows(own // pair - 1)

    for at in range(C - 1):
        tiles = (at + 1) * (own + (R - 1) * early)

        @pl.when(c == at)
        def _():
            sent(right_sem.at[0], tiles)

        @pl.when(C - 1 - c == at)
        def _():
            sent(left_sem.at[0], tiles)

    for d in range(R - 1):
        sent(row_sem.at[d], own + (C - 1) * (own - early))
    for d, other in enumerate(twins + [partner]):
        low_move(low.at[l], send_low.at[d], recv_low.at[0, 0], other).wait_send()
    for d, other in enumerate(twins):
        low_move(low.at[other], relay_low.at[d], recv_low.at[0, 0], partner).wait_send()


def on_device(R, C, L, density, tile_cols, out_cols):
    own, _, bs, _ = density.shape
    kq = out_cols.shape[2]
    pieces = kq
    groups = R * C
    chunks = len(chunk_plan(own))
    dma = pltpu.SemaphoreType.DMA
    bf16, f32 = jnp.bfloat16, jnp.float32
    tiles = 2 * groups * own + own * L + 2 * own * kq + own * L * kq + own * kq
    vmem = tiles * bs * bs * 2 + 2 * 2**20
    tc, oc = tile_cols.T, out_cols.transpose(1, 2, 0)
    tc, oc = (pltpu.with_memory_space_constraint(part, pltpu.HBM) for part in (tc, oc))
    return pl.pallas_call(
        functools.partial(purify_kernel, R, C, L),
        out_shape=jax.ShapeDtypeStruct((own, 1, kq, bs, bs), bf16),
        in_specs=[
            pl.BlockSpec(memory_space=pltpu.HBM),
            pl.BlockSpec(memory_space=pltpu.HBM),
            pl.BlockSpec(memory_space=pltpu.HBM),
        ],
        out_specs=pl.BlockSpec(memory_space=pltpu.VMEM),
        scratch_shapes=[
            [pltpu.VMEM((groups * own, bs // pieces, bs), bf16) for _ in range(pieces)],
            pltpu.VMEM((groups * own, bs, bs), bf16),
            pltpu.VMEM((own, L, bs, bs), bf16),
            pltpu.VMEM((own, bs, kq * bs), f32),
            pltpu.VMEM((L, pieces, own, bs, bs), bf16),
            dma((4,)),
            dma((groups, pieces)),
            dma((C, pieces, chunks - 1)),
            dma((pieces,)),
            dma((1,)),
            dma((1,)),
            dma((max(R - 1, 1),)),
            dma((pieces - 1, L)),
            dma((L, own // 2)),
            dma((L // 2,)),
            dma((max(L // 2 - 1, 1),)),
            pltpu.SMEM(tc.shape, jnp.int32),
            pltpu.SMEM(oc.shape, jnp.int32),
        ],
        compiler_params=pltpu.CompilerParams(
            collective_id=0, has_side_effects=True, vmem_limit_bytes=max(vmem, 51 * 2**20)
        ),
    )(density, tc, oc)


def solution(mesh):
    R, C, L = (mesh.shape[name] for name in ("row", "col", "layer"))
    placed = (P(("row", "col"), None, None, None), P(), P(("row", "col"), None, None))
    return jax.shard_map(
        functools.partial(on_device, R, C, L),
        mesh=mesh,
        in_specs=placed,
        out_specs=P(("row", "col"), "layer", None, None, None),
        check_vma=False,
    )
```
